32 devices in a mesh: ctx: 8 (over z, core), tp: 4 (over y, x).
Axes of the slice: x: 2, y: 2, z: 4, core: 2. Of those that a mesh axis runs over, the one named last changes fastest.
Arguments:
- query_in: bfloat16 [8192, 1024], P(('ctx', 'tp')), may hold values from -6 to 6
- key_in: bfloat16 [8192, 1024], P(('ctx', 'tp')), may hold values from -6 to 6
- value_in: bfloat16 [8192, 1024], P(('ctx', 'tp')), may hold values from -6 to 6
- lookback: int32 [64], replicated, may hold values from 0 to 3, as said below
- out_grad: bfloat16 [1024, 8192], P('tp', 'ctx'), may hold values from -6 to 6
Outputs:
- attention: bfloat16 [1024, 8192], P('tp', 'ctx')
- grad_query: bfloat16 [1024, 8192], P('tp', 'ctx')
- grad_key: bfloat16 [1024, 8192], P('tp', 'ctx')
- grad_value: bfloat16 [1024, 8192], P('tp', 'ctx')
The draws below stay inside these ranges and needn't reach their ends.
Inputs may be any that keep to these rules, and one draw needn't show every extreme that they name: The queries of frame f see the keys of frames f - lookback[f] to f; some frame has 3 and some frame has 0.
All inputs are finite; a program needn't handle non-finite values.
Results may differ from the reference program's by a relative error of at most 0.02.
Values may be sent and summed in bfloat16 or wider, within the bound.
A program may use at most 64 MiB of HBM per device.

```python
import jax
import jax.numpy as jnp
from jax import lax

D = 1024
H = 16
HEAD = 64
CH = 128
FPC = 4
W = 3
FRAMES = 64
TOKENS = 8192
N_CTX = 8


def draw_query_in(key, part):
    drawn = jnp.clip(jax.random.normal(jax.random.fold_in(key, 21), (TOKENS, D), jnp.float32), -5.0, 5.0)
    return drawn.astype(jnp.bfloat16)


def draw_key_in(key, part):
    drawn = jnp.clip(jax.random.normal(jax.random.fold_in(key, 31), (TOKENS, D), jnp.float32), -5.0, 5.0)
    return drawn.astype(jnp.bfloat16)


def draw_lookback(key, part):
    windows = jax.random.randint(jax.random.fold_in(key, 41), (FRAMES,), 0, W + 1)
    shuffled = jax.random.permutation(jax.random.fold_in(key, 42), FRAMES)
    windows = windows.at[shuffled[0]].set(W)
    windows = windows.at[shuffled[1]].set(0)
    return windows.astype(jnp.int32)


def block_scale(key, dims, split, low, top_value):
    factor_of = 1.0
    for dim, parts in split:
        draws = jax.random.uniform(jax.random.fold_in(jax.random.fold_in(key, 6), dim), (parts,), jnp.float32, low / len(split), top_value / len(split))
        factor_of = factor_of * jnp.repeat(jnp.exp(draws), dims[dim] // parts).reshape((-1,) + (1,) * (len(dims) - 1 - dim))
    return factor_of


def bell_draw(rng, dims, deviation, bound, pieces=(), held_as=jnp.bfloat16):
    values = jax.random.normal(rng, dims, jnp.float32) * deviation
    if len(pieces) > 0:
        values = block_scale(rng, dims, pieces, -0.22, 0.18) * values
    return jnp.clip(values, min=-bound, max=bound).astype(held_as)


def setup_inputs(seed: int = 0) -> dict:
    key_of = jax.random.split(jax.random.key(seed), 6)
    query_in = draw_query_in(jax.random.fold_in(key_of[5], 71), 0)
    key_in = draw_key_in(jax.random.fold_in(key_of[5], 71), 0)
    value_in = bell_draw(key_of[2], (TOKENS, D), 1.0, 6.0, ((0, 32),))
    lookback = draw_lookback(jax.random.fold_in(key_of[5], 71), 0)
    out_grad = bell_draw(key_of[4], (D, TOKENS), 1.0, 6.0, ((0, 4), (1, 8)))
    return {"query_in": query_in, "key_in": key_in, "value_in": value_in, "lookback": lookback, "out_grad": out_grad}


SCORE_SCALE = 0.125


def reference(query_in, key_in, value_in, lookback, out_grad):
    frames = FRAMES
    slot_total = 2 * N_CTX
    group_ids = jnp.arange(slot_total, dtype=jnp.int32)
    source_slot = jnp.where(group_ids < N_CTX, 2 * group_ids, 2 * (slot_total - 1 - group_ids) + 1)
    stored_group = jnp.where(group_ids % 2 == 0, group_ids // 2, slot_total - 1 - group_ids // 2)
    frame_ids = jnp.arange(frames, dtype=jnp.int32)

    def by_frame(array):
        return array.reshape(slot_total, FPC * CH, H, HEAD)[source_slot].reshape(frames, CH, H, HEAD).astype(jnp.float32)

    query_all = by_frame(query_in)
    key_all = by_frame(key_in)
    value_all = by_frame(value_in)
    grad_all = by_frame(out_grad.T)
    offsets = jnp.arange(W + 1, dtype=jnp.int32)

    def window_rows(array, indices):
        return array[indices].reshape((W + 1) * CH, H, HEAD)

    def forward(frame):
        nearby = frame - W + offsets
        permitted = (nearby >= 0) & (nearby >= frame - lookback[frame])
        row_keep = jnp.repeat(permitted, CH)
        indices = jnp.clip(nearby, 0, frames - 1).astype(jnp.int32)
        near_keys = window_rows(key_all, indices)
        near_values = window_rows(value_all, indices)
        raw_scores = jnp.einsum("qhd,khd->hqk", query_all[frame], near_keys) * SCORE_SCALE
        masked = jnp.where(row_keep[None, None, :], raw_scores, -jnp.inf)
        top_score = jnp.max(masked, -1, keepdims=True)
        log_total = top_score + jnp.log(jnp.sum(jnp.exp(masked - top_score), -1, keepdims=True))
        probability = jnp.exp(masked - log_total)
        weights = lax.optimization_barrier(probability.astype(jnp.bfloat16)).astype(jnp.float32)
        output = jnp.einsum("hqk,khd->qhd", weights, near_values).astype(jnp.bfloat16)
        output_full = lax.optimization_barrier(output).astype(jnp.float32)
        inner_sum = jnp.sum(grad_all[frame] * output_full, -1).T
        grad_prob = jnp.einsum("qhd,khd->hqk", grad_all[frame], near_values)
        grad_score = (probability * (grad_prob - inner_sum[:, :, None])).astype(jnp.bfloat16)
        grad_score = lax.optimization_barrier(grad_score).astype(jnp.float32)
        grad_query = (jnp.einsum("hqk,khd->qhd", grad_score, near_keys) * SCORE_SCALE).astype(jnp.bfloat16)
        return output, grad_query, log_total[:, :, 0], inner_sum

    outputs, grad_queries, log_totals, inner_sums = lax.map(forward, frame_ids)

    def backward(key_frame):
        nearby = key_frame + offsets
        indices = jnp.clip(nearby, 0, frames - 1).astype(jnp.int32)
        windows = lookback[indices]
        permitted = (nearby <= frames - 1) & (key_frame >= nearby - windows)
        row_keep = jnp.repeat(permitted, CH)
        near_queries = window_rows(query_all, indices)
        near_grads = window_rows(grad_all, indices)
        near_log = jnp.transpose(log_totals[indices], (1, 0, 2)).reshape(H, (W + 1) * CH)
        near_inner = jnp.transpose(inner_sums[indices], (1, 0, 2)).reshape(H, (W + 1) * CH)
        raw_scores = jnp.einsum("qhd,khd->hqk", near_queries, key_all[key_frame]) * SCORE_SCALE
        masked = jnp.where(row_keep[None, :, None], raw_scores, -jnp.inf)
        probability = jnp.exp(masked - near_log[:, :, None])
        weights = lax.optimization_barrier(probability.astype(jnp.bfloat16)).astype(jnp.float32)
        grad_value = jnp.einsum("hqk,qhd->khd", weights, near_grads).astype(jnp.bfloat16)
        grad_prob = jnp.einsum("qhd,khd->hqk", near_grads, value_all[key_frame])
        grad_score = (probability * (grad_prob - near_inner[:, :, None])).astype(jnp.bfloat16)
        grad_score = lax.optimization_barrier(grad_score).astype(jnp.float32)
        grad_key = (jnp.einsum("hqk,qhd->khd", grad_score, near_queries) * SCORE_SCALE).astype(jnp.bfloat16)
        return grad_key, grad_value

    grad_keys, grad_values = lax.map(backward, frame_ids)

    def to_stored(array):
        return array.reshape(slot_total, FPC * CH, H * HEAD)[stored_group].reshape(TOKENS, D).T

    return (to_stored(outputs), to_stored(grad_queries), to_stored(grad_keys), to_stored(grad_values))
```

```python
import functools
from functools import reduce

import jax
import jax.numpy as jnp
from jax import lax
from jax.experimental import pallas as pl
from jax.experimental.pallas import tpu as pltpu
from jax.sharding import PartitionSpec as P

HEAD = 64
FPC = 4
W = 3
CH = 128
PAIR = 2 * HEAD
GROUP = FPC * CH
TAIL = W * CH
EXT = TAIL + GROUP
SPAN = (W + 1) * CH
SCALE = 0.125
MESH = pl.DeviceIdType.MESH
NT = (((1,), (1,)), ((), ()))
NN = (((1,), (0,)), ((), ()))
F32 = jnp.float32
BF16 = jnp.bfloat16


def mm(a, b, dims):
    return lax.dot_general(a, b, dims, preferred_element_type=F32)


def kernel(
    tp, ctx, q_hbm, k_hbm, v_hbm, look, og,
    att, gq, gk, gv,
    qbuf, kext, vext, kt, vt, acck, accv, gsend, gret,
    own_sem, send_sem, recv_sem, tsend, trecv, gssem, grsem,
):
    rows, width = q_hbm.shape
    feats = width // tp
    pairs = feats // PAIR
    me = lax.axis_index("tp")
    d = lax.axis_index("ctx")
    last = ctx - 1
    groups = 2 * ctx

    barrier = pltpu.get_barrier_semaphore()
    for o in range(1, tp):
        pl.semaphore_signal(barrier, inc=1, device_id={"tp": lax.rem(me + o, tp)}, device_id_type=MESH)

    @pl.when(d > 0)
    def _():
        pl.semaphore_signal(barrier, inc=1, device_id={"ctx": d - 1}, device_id_type=MESH)

    @pl.when(d < last)
    def _():
        pl.semaphore_signal(barrier, inc=1, device_id={"ctx": d + 1}, device_id_type=MESH)

    def ext_row(p):
        return pl.multiple_of(p * rows + TAIL + TAIL * (p // (tp // 2)), CH)

    arrays = ((k_hbm, kext), (v_hbm, vext), (q_hbm, qbuf))

    def dst_row(a):
        return pl.multiple_of(me * rows, CH) if a == 2 else ext_row(me)

    def own_copy(a, hp):
        src, dst = arrays[a]
        return pltpu.make_async_copy(
            src.at[:, pl.ds(pl.multiple_of(me * feats + hp * PAIR, PAIR), PAIR)],
            dst.at[pl.ds(dst_row(a), rows), pl.ds(hp * PAIR, PAIR)],
            own_sem.at[a, hp],
        )

    def peer_copy(a, hp, o):
        src, dst = arrays[a]
        to = lax.rem(me + o, tp)
        return pltpu.make_async_remote_copy(
            src_ref=src.at[:, pl.ds(pl.multiple_of(to * feats + hp * PAIR, PAIR), PAIR)],
            dst_ref=dst.at[pl.ds(dst_row(a), rows), pl.ds(hp * PAIR, PAIR)],
            send_sem=send_sem.at[a, hp, o - 1],
            recv_sem=recv_sem.at[a, hp, o - 1],
            device_id={"tp": to},
            device_id_type=MESH,
        )

    for hp in range(pairs):
        for a in range(3):
            own_copy(a, hp).start()
    amount = tp - 1 + jnp.where(d > 0, 1, 0) + jnp.where(d < last, 1, 0)
    pl.semaphore_wait(barrier, amount)
    for hp in range(pairs):
        for a in range(3):
            for o in range(1, tp):
                peer_copy(a, hp, o).start()

    def arrived(a, hp):
        own_copy(a, hp).wait()
        for o in range(1, tp):
            peer_copy(a, hp, o).wait_recv()

    def tail_copy(a, hp, g):
        buf = arrays[a][1]
        return pltpu.make_async_remote_copy(
            src_ref=buf.at[pl.ds(g * EXT + EXT - TAIL, TAIL), pl.ds(hp * PAIR, PAIR)],
            dst_ref=buf.at[pl.ds(g * EXT, TAIL), pl.ds(hp * PAIR, PAIR)],
            send_sem=tsend.at[a, hp, g],
            recv_sem=trecv.at[a, hp, g],
            device_id={"ctx": d + 1 - 2 * g},
            device_id_type=MESH,
        )

    def grad_copy(a, hp, g):
        return pltpu.make_async_remote_copy(
            src_ref=gsend.at[a, g, pl.ds(hp * PAIR, PAIR)],
            dst_ref=gret.at[a, g, pl.ds(hp * PAIR, PAIR)],
            send_sem=gssem.at[a, hp, g],
            recv_sem=grsem.at[a, hp, g],
            device_id={"ctx": d - 1 + 2 * g},
            device_id_type=MESH,
        )

    def forward_tails(a, hp):
        lanes = slice(hp * PAIR, hp * PAIR + PAIR)
        buf = arrays[a][1]

        @pl.when(d < last)
        def _():
            tail_copy(a, hp, 0).start()

        @pl.when(d > 0)
        def _():
            tail_copy(a, hp, 1).start()

        @pl.when(d == 0)
        def _():
            buf[0:TAIL, lanes] = jnp.zeros((TAIL, PAIR), BF16)

        @pl.when(d == last)
        def _():
            buf[EXT : EXT + TAIL, lanes] = buf[EXT - TAIL : EXT, lanes]

    def tails_arrived(a, hp):
        @pl.when(d > 0)
        def _():
            tail_copy(a, hp, 0).wait_recv()

        @pl.when(d < last)
        def _():
            tail_copy(a, hp, 1).wait_recv()

    def turn(a, hp, first, stop):
        buf, out = ((kext, kt), (vext, vt))[a]
        lanes = slice(hp * PAIR, hp * PAIR + PAIR)
        for g in range(2):
            at = slice(g * EXT + first * CH, g * EXT + stop * CH)
            out[lanes, at] = buf[at, lanes].T

    def item(hp, g, f):
        lanes = slice(hp * PAIR, hp * PAIR + PAIR)
        base = pl.multiple_of(g * EXT + f * CH, CH)
        tok = pl.multiple_of(g * GROUP + f * CH, CH)
        frame = jnp.where(g == 0, d, groups - 1 - d) * FPC + f
        back = look[frame]
        k = kext[pl.ds(base, SPAN), lanes]
        v = vext[pl.ds(base, SPAN), lanes]
        q = qbuf[pl.ds(tok, CH), lanes]
        lane = lax.broadcasted_iota(jnp.int32, (CH, PAIR), 1)
        feat = lax.broadcasted_iota(jnp.int32, (PAIR, CH), 0)
        zero = jnp.zeros((CH, PAIR), BF16)
        q2 = jnp.concatenate([jnp.where(lane < HEAD, q, zero), jnp.where(lane < HEAD, zero, q)], 0)
        s = mm(k, q2 * jnp.asarray(SCALE, BF16), NT)
        parts = []
        for j in range(W + 1):
            part = s[j * CH : (j + 1) * CH]
            if j < W:
                seen = jnp.where(frame - W + j >= 0, W - j, FPC * groups)
                part = part + jnp.where(seen <= back, 0.0, -1e30)
            parts.append(part)
        s = jnp.concatenate(parts, 0)
        e = jnp.exp(s - jnp.max(s, 0, keepdims=True))
        p = e * (1.0 / jnp.sum(e, 0, keepdims=True))
        pb = p.astype(BF16)
        do = og[lanes, pl.ds(tok, CH)]
        do2 = jnp.concatenate([jnp.where(feat < HEAD, do, zero), jnp.where(feat < HEAD, zero, do)], 1)
        dp = mm(v, do2, NN)
        o2 = mm(vt[lanes, pl.ds(base, SPAN)], pb, NN)
        out = jnp.where(feat < HEAD, o2[:, :CH], o2[:, CH:]).astype(BF16)
        att[lanes, pl.ds(tok, CH)] = out
        prod = do.astype(F32) * out.astype(F32)
        inner = jnp.concatenate(
            [jnp.sum(prod[:HEAD], 0, keepdims=True), jnp.sum(prod[HEAD:], 0, keepdims=True)], 1
        )
        ds = (p * (dp - inner)).astype(BF16)
        dq2 = mm(kt[lanes, pl.ds(base, SPAN)], ds, NN)
        gq[lanes, pl.ds(tok, CH)] = (
            jnp.where(feat < HEAD, dq2[:, :CH], dq2[:, CH:]) * SCALE
        ).astype(BF16)
        acck[lanes, pl.ds(base, SPAN)] += mm(q2.T, ds, NT)
        accv[lanes, pl.ds(base, SPAN)] += mm(do2, pb, NT)

    def send_grads(hp):
        lanes = slice(hp * PAIR, hp * PAIR + PAIR)
        for g in range(2):
            gsend[0, g, lanes] = (acck[lanes, g * EXT : g * EXT + TAIL] * SCALE).astype(BF16)
            gsend[1, g, lanes] = accv[lanes, g * EXT : g * EXT + TAIL].astype(BF16)
        for a in range(2):

            @pl.when(d > 0)
            def _():
                grad_copy(a, hp, 0).start()

            @pl.when(d < last)
            def _():
                grad_copy(a, hp, 1).start()

            @pl.when(d == 0)
            def _():
                gret[a, 1, lanes] = jnp.zeros((PAIR, TAIL), BF16)

            @pl.when(d == last)
            def _():
                gret[a, 0, lanes] = gsend[a, 1, lanes]

    def finish(hp):
        lanes = slice(hp * PAIR, hp * PAIR + PAIR)
        for a in range(2):

            @pl.when(d < last)
            def _():
                grad_copy(a, hp, 0).wait_recv()

            @pl.when(d > 0)
            def _():
                grad_copy(a, hp, 1).wait_recv()

            acc, out = ((acck, gk), (accv, gv))[a]
            for g in range(2):
                own = acc[lanes, g * EXT + TAIL : (g + 1) * EXT]
                if a == 0:
                    own = own * SCALE
                own_tail = own[:, GROUP - TAIL :] + gret[a, g, lanes].astype(F32)
                out[lanes, g * GROUP : (g + 1) * GROUP - TAIL] = own[:, : GROUP - TAIL].astype(BF16)
                out[lanes, (g + 1) * GROUP - TAIL : (g + 1) * GROUP] = own_tail.astype(BF16)

    acck[...] = jnp.zeros_like(acck)
    accv[...] = jnp.zeros_like(accv)

    def receive(hp):
        for a in range(2):
            arrived(a, hp)
            forward_tails(a, hp)
            turn(a, hp, W, W + FPC)
        arrived(2, hp)
        for a in range(2):
            tails_arrived(a, hp)
            turn(a, hp, 0, W)

    for hp in range(pairs):
        receive(hp)

        @pl.loop(0, W)
        def _(f):
            for g in range(2):
                item(hp, g, f)

        send_grads(hp)
        for g in range(2):
            item(hp, g, W)
        if hp > 0:
            finish(hp - 1)
    finish(pairs - 1)

    for hp in range(pairs):
        for a in range(3):
            for o in range(1, tp):
                peer_copy(a, hp, o).wait_send()
        for a in range(2):

            @pl.when(d < last)
            def _():
                tail_copy(a, hp, 0).wait_send()
                grad_copy(a, hp, 1).wait_send()

            @pl.when(d > 0)
            def _():
                tail_copy(a, hp, 1).wait_send()
                grad_copy(a, hp, 0).wait_send()


def on_device(tp, ctx, query_in, key_in, value_in, lookback, out_grad):
    feats, tokens = out_grad.shape
    pairs = feats // PAIR
    dma = pltpu.SemaphoreType.DMA
    vmem = pl.BlockSpec(memory_space=pltpu.VMEM)
    anywhere = pl.BlockSpec(memory_space=pl.ANY)
    return pl.pallas_call(
        functools.partial(kernel, tp, ctx),
        out_shape=[jax.ShapeDtypeStruct((feats, tokens), BF16)] * 4,
        in_specs=[anywhere] * 3 + [pl.BlockSpec(memory_space=pltpu.SMEM), vmem],
        out_specs=[vmem] * 4,
        scratch_shapes=[
            pltpu.VMEM((2 * GROUP, feats), BF16),
            pltpu.VMEM((2 * EXT, feats), BF16),
            pltpu.VMEM((2 * EXT, feats), BF16),
            pltpu.VMEM((feats, 2 * EXT), BF16),
            pltpu.VMEM((feats, 2 * EXT), BF16),
            pltpu.VMEM((feats, 2 * EXT), F32),
            pltpu.VMEM((feats, 2 * EXT), F32),
            pltpu.VMEM((2, 2, feats, TAIL), BF16),
            pltpu.VMEM((2, 2, feats, TAIL), BF16),
            dma((3, pairs)),
            dma((3, pairs, tp - 1)),
            dma((3, pairs, tp - 1)),
            dma((2, pairs, 2)),
            dma((2, pairs, 2)),
            dma((2, pairs, 2)),
            dma((2, pairs, 2)),
        ],
        compiler_params=pltpu.CompilerParams(
            collective_id=0, has_side_effects=True, vmem_limit_bytes=48 << 20
        ),
    )(query_in, key_in, value_in, lookback, out_grad)


SCORE_SCALE = 0.125


def from_behind(shard, axis, by):
    length = lax.axis_size(axis)
    pairs = [(i, i + by) for i in range(length) if 0 <= i + by < length]
    return lax.ppermute(shard, axis, pairs)


def masked_scores(query_block, key_block, allowed):
    raw_scores = (
        jnp.einsum("fqhd,fkhd->fhqk", query_block, key_block, preferred_element_type=jnp.float32)
        * SCORE_SCALE
    )
    return jnp.where(allowed[:, None, None, None], raw_scores, -jnp.inf)


def stats_block(inputs, allowed):
    query_block, key_block = inputs
    masked = masked_scores(query_block, key_block, allowed)
    block_max = jnp.max(masked, -1)
    safe_max = jnp.where(block_max == -jnp.inf, 0.0, block_max)
    return (block_max, jnp.sum(jnp.exp(masked - safe_max[..., None]), -1))


def output_block(inputs, allowed):
    query_block, key_block, value_block, log_block = inputs
    weights = jnp.exp(masked_scores(query_block, key_block, allowed) - log_block[..., None]).astype(
        jnp.bfloat16
    )
    return jnp.einsum("fhqk,fkhd->fqhd", weights, value_block, preferred_element_type=jnp.float32)


def back_block(inputs, allowed):
    query_block, grad_block, log_block, inner_block, key_block, value_block = inputs
    probability = jnp.exp(masked_scores(query_block, key_block, allowed) - log_block[..., None])
    grad_prob = jnp.einsum(
        "fqhd,fkhd->fhqk", grad_block, value_block, preferred_element_type=jnp.float32
    )
    grad_score = (probability * (grad_prob - inner_block[..., None])).astype(jnp.bfloat16)
    key_part = (
        jnp.einsum("fhqk,fqhd->fkhd", grad_score, query_block, preferred_element_type=jnp.float32)
        * SCORE_SCALE
    )
    value_part = jnp.einsum(
        "fhqk,fqhd->fkhd",
        probability.astype(jnp.bfloat16),
        grad_block,
        preferred_element_type=jnp.float32,
    )
    query_part = (
        jnp.einsum("fhqk,fkhd->fqhd", grad_score, key_block, preferred_element_type=jnp.float32)
        * SCORE_SCALE
    )
    return (query_part, key_part, value_part)


def general(query_in, key_in, value_in, lookback, out_grad):
    query_rows, key_rows, value_rows = (
        lax.all_to_all(query_in, "tp", split_axis=1, concat_axis=0, tiled=True),
        lax.all_to_all(key_in, "tp", split_axis=1, concat_axis=0, tiled=True),
        lax.all_to_all(value_in, "tp", split_axis=1, concat_axis=0, tiled=True),
    )
    row_count = query_rows.shape[0]
    frame_rows = row_count // (2 * FPC)
    head_count = out_grad.shape[0] // HEAD
    ctx_count = lax.axis_size("ctx")
    group_total = 2 * ctx_count
    device = lax.axis_index("ctx")
    last_device = device == ctx_count - 1
    layout = (2, FPC, frame_rows, head_count, HEAD)
    query_heads = query_rows.reshape(layout)
    grad_heads = out_grad.T.reshape(layout)
    local_pair = jnp.stack([key_rows.reshape(layout), value_rows.reshape(layout)], 4)
    tail_width = head_count * 2 * HEAD
    low_tail = local_pair[0, FPC - W :].reshape(W * frame_rows, tail_width)
    high_tail = local_pair[1, FPC - W :].reshape(W * frame_rows, tail_width)
    below = from_behind(low_tail, "ctx", 1)
    above = from_behind(high_tail, "ctx", -1)
    above = jnp.where(last_device, low_tail, above)
    tails = jnp.stack([below, above]).reshape(2, W, frame_rows, head_count, 2, HEAD)
    extended = jnp.concatenate([tails, local_pair], 1)
    frame_ids = jnp.arange(group_total * FPC, dtype=jnp.int32)
    group_pair = jnp.stack([device, group_total - 1 - device])
    query_frame = group_pair[:, None] * FPC + jnp.arange(FPC, dtype=jnp.int32)[None, :]
    query_look = jnp.sum(jnp.where(query_frame[..., None] == frame_ids, lookback, 0), -1)
    permits = []
    for offset in range(W + 1):
        key_frame = query_frame - W + offset
        permits.append(
            ((key_frame >= 0) & (key_frame >= query_frame - query_look)).reshape(2 * FPC)
        )

    def window(offset):
        pair = extended[:, offset : offset + FPC].reshape(2 * FPC, frame_rows, head_count, 2, HEAD)
        return (pair[:, :, :, 0], pair[:, :, :, 1])

    flat_query = query_heads.reshape(2 * FPC, frame_rows, head_count, HEAD)
    flat_grad = grad_heads.reshape(2 * FPC, frame_rows, head_count, HEAD)
    block_stats = [
        stats_block((flat_query, window(offset)[0]), permits[offset]) for offset in range(W + 1)
    ]
    total_max = reduce(jnp.maximum, [entry[0] for entry in block_stats])
    total_sum = jnp.zeros_like(total_max)
    for entry in block_stats:
        total_sum = total_sum + entry[1] * jnp.exp(entry[0] - total_max)
    log_total = total_max + jnp.log(total_sum)
    summed = jnp.zeros((2 * FPC, frame_rows, head_count, HEAD), jnp.float32)
    for offset in range(W + 1):
        keys, values = window(offset)
        summed = summed + output_block((flat_query, keys, values, log_total), permits[offset])
    attention = summed.astype(jnp.bfloat16)
    inner_sum = jnp.transpose(
        jnp.sum(flat_grad.astype(jnp.float32) * attention.astype(jnp.float32), -1), (0, 2, 1)
    )

    def pad_frames(part, first, stop, length):
        shaped = part.reshape((2, stop - first) + part.shape[1:])
        return jnp.pad(shaped, ((0, 0), (first, length - stop), (0, 0), (0, 0), (0, 0)))

    grad_query = jnp.zeros((2 * FPC, frame_rows, head_count, HEAD), jnp.float32)
    key_total = jnp.zeros((2, W + FPC, frame_rows, head_count, HEAD), jnp.float32)
    value_total = jnp.zeros((2, W + FPC, frame_rows, head_count, HEAD), jnp.float32)
    for offset in range(W + 1):
        keys, values = window(offset)
        query_part, key_part, value_part = back_block(
            (flat_query, flat_grad, log_total, inner_sum, keys, values), permits[offset]
        )
        grad_query = grad_query + query_part
        key_total = key_total + pad_frames(key_part, offset, offset + FPC, W + FPC)
        value_total = value_total + pad_frames(value_part, offset, offset + FPC, W + FPC)
    tail_grads = jnp.stack([key_total[:, :W], value_total[:, :W]], 4).reshape(
        2, W * frame_rows, tail_width
    )
    from_above = from_behind(tail_grads[0].astype(jnp.bfloat16), "ctx", -1).astype(jnp.float32)
    from_below = from_behind(tail_grads[1].astype(jnp.bfloat16), "ctx", 1).astype(jnp.float32)
    returned = jnp.stack(
        [from_above + jnp.where(last_device, tail_grads[1], 0.0), from_below]
    ).reshape(2, W, frame_rows, head_count, 2, HEAD)
    tail_pad = ((0, 0), (FPC - W, 0), (0, 0), (0, 0), (0, 0))
    own_key = key_total[:, W:] + jnp.pad(returned[:, :, :, :, 0], tail_pad)
    own_value = value_total[:, W:] + jnp.pad(returned[:, :, :, :, 1], tail_pad)
    width = head_count * HEAD

    def finish(array):
        return array.astype(jnp.bfloat16).reshape(row_count, width).T

    return (
        attention.reshape(row_count, width).T,
        finish(grad_query),
        finish(own_key),
        finish(own_value),
    )


def solution(mesh):
    tp, ctx = mesh.shape["tp"], mesh.shape["ctx"]
    rows = P(("ctx", "tp"), None)
    out = P("tp", "ctx")

    def step(*args):
        if args[4].shape[0] % PAIR or args[0].shape[0] % CH:
            return general(*args)
        return on_device(tp, ctx, *args)

    return jax.shard_map(
        step,
        mesh=mesh,
        in_specs=(rows, rows, rows, P(), out),
        out_specs=(out,) * 4,
        check_vma=False,
    )
```

```python
import functools
from functools import reduce

import jax
import jax.numpy as jnp
from jax import lax
from jax.experimental import pallas as pl
from jax.experimental.pallas import tpu as pltpu
from jax.sharding import PartitionSpec as P

HEAD = 64
FPC = 4
W = 3
CH = 128
PAIR = 2 * HEAD
GROUP = FPC * CH
TAIL = W * CH
EXT = TAIL + GROUP
SPAN = (W + 1) * CH
SCALE = 0.125
EARLY = 2
MESH = pl.DeviceIdType.MESH
NT = (((1,), (1,)), ((), ()))
NN = (((1,), (0,)), ((), ()))
F32 = jnp.float32
BF16 = jnp.bfloat16


def mm(a, b, dims):
    return lax.dot_general(a, b, dims, preferred_element_type=F32)


def kernel(
    tp, ctx, q_hbm, k_hbm, v_hbm, look_hbm, og_hbm,
    att_out, gq_out, gk_out, gv_out,
    att, gq, gk, gv,
    look, og, qbuf, kext, vext, kt, vt, acck, accv, gsend, gret,
    in_sem, out_sem, own_sem, send_sem, recv_sem, tsend, trecv, gssem, grsem,
):
    rows, width = q_hbm.shape
    feats = width // tp
    pairs = feats // PAIR
    me = lax.axis_index("tp")
    d = lax.axis_index("ctx")
    last = ctx - 1
    groups = 2 * ctx

    barrier = pltpu.get_barrier_semaphore()
    for o in range(1, tp):
        pl.semaphore_signal(barrier, inc=1, device_id={"tp": lax.rem(me + o, tp)}, device_id_type=MESH)

    @pl.when(d > 0)
    def _():
        pl.semaphore_signal(barrier, inc=1, device_id={"ctx": d - 1}, device_id_type=MESH)

    @pl.when(d < last)
    def _():
        pl.semaphore_signal(barrier, inc=1, device_id={"ctx": d + 1}, device_id_type=MESH)

    def ext_row(p):
        return pl.multiple_of(p * rows + TAIL + TAIL * (p // (tp // 2)), CH)

    arrays = ((k_hbm, kext), (v_hbm, vext), (q_hbm, qbuf))

    def dst_row(a):
        return pl.multiple_of(me * rows, CH) if a == 2 else ext_row(me)

    def own_copy(a, hp):
        src, dst = arrays[a]
        return pltpu.make_async_copy(
            src.at[:, pl.ds(pl.multiple_of(me * feats + hp * PAIR, PAIR), PAIR)],
            dst.at[pl.ds(dst_row(a), rows), pl.ds(hp * PAIR, PAIR)],
            own_sem.at[a, hp],
        )

    def peer_copy(a, hp, o):
        src, dst = arrays[a]
        to = lax.rem(me + o, tp)
        return pltpu.make_async_remote_copy(
            src_ref=src.at[:, pl.ds(pl.multiple_of(to * feats + hp * PAIR, PAIR), PAIR)],
            dst_ref=dst.at[pl.ds(dst_row(a), rows), pl.ds(hp * PAIR, PAIR)],
            send_sem=send_sem.at[a, hp, o - 1],
            recv_sem=recv_sem.at[a, hp, o - 1],
            device_id={"tp": to},
            device_id_type=MESH,
        )

    look_copy = pltpu.make_async_copy(look_hbm, look, in_sem.at[0])
    og_copy = pltpu.make_async_copy(og_hbm, og, in_sem.at[1])
    amount = tp - 1 + jnp.where(d > 0, 1, 0) + jnp.where(d < last, 1, 0)
    pl.semaphore_wait(barrier, amount)

    def send(hp):
        for a in range(3):
            for o in range(1, tp):
                peer_copy(a, hp, o).start()

    send(0)
    for hp in range(pairs):
        for a in range(3):
            own_copy(a, hp).start()
    look_copy.start()
    og_copy.start()

    def arrived(a, hp):
        own_copy(a, hp).wait()
        for o in range(1, tp):
            peer_copy(a, hp, o).wait_recv()

    def tail_copy(a, hp, g):
        buf = arrays[a][1]
        return pltpu.make_async_remote_copy(
            src_ref=buf.at[pl.ds(g * EXT + EXT - TAIL, TAIL), pl.ds(hp * PAIR, PAIR)],
            dst_ref=buf.at[pl.ds(g * EXT, TAIL), pl.ds(hp * PAIR, PAIR)],
            send_sem=tsend.at[a, hp, g],
            recv_sem=trecv.at[a, hp, g],
            device_id={"ctx": d + 1 - 2 * g},
            device_id_type=MESH,
        )

    def grad_copy(a, hp, g):
        return pltpu.make_async_remote_copy(
            src_ref=gsend.at[a, g, pl.ds(hp * PAIR, PAIR)],
            dst_ref=gret.at[a, g, pl.ds(hp * PAIR, PAIR)],
            send_sem=gssem.at[a, hp, g],
            recv_sem=grsem.at[a, hp, g],
            device_id={"ctx": d - 1 + 2 * g},
            device_id_type=MESH,
        )

    def forward_tails(a, hp):
        lanes = slice(hp * PAIR, hp * PAIR + PAIR)
        buf = arrays[a][1]

        @pl.when(d < last)
        def _():
            tail_copy(a, hp, 0).start()

        @pl.when(d > 0)
        def _():
            tail_copy(a, hp, 1).start()

        @pl.when(d == 0)
        def _():
            buf[0:TAIL, lanes] = jnp.zeros((TAIL, PAIR), BF16)

        @pl.when(d == last)
        def _():
            buf[EXT : EXT + TAIL, lanes] = buf[EXT - TAIL : EXT, lanes]

    def tails_arrived(a, hp):
        @pl.when(d > 0)
        def _():
            tail_copy(a, hp, 0).wait_recv()

        @pl.when(d < last)
        def _():
            tail_copy(a, hp, 1).wait_recv()

    def turn(a, hp, first, stop):
        buf, out = ((kext, kt), (vext, vt))[a]
        lanes = slice(hp * PAIR, hp * PAIR + PAIR)
        for g in range(2):
            at = slice(g * EXT + first * CH, g * EXT + stop * CH)
            out[lanes, at] = buf[at, lanes].T

    def item(hp, g, f):
        lanes = slice(hp * PAIR, hp * PAIR + PAIR)
        base = pl.multiple_of(g * EXT + f * CH, CH)
        tok = pl.multiple_of(g * GROUP + f * CH, CH)
        frame = jnp.where(g == 0, d, groups - 1 - d) * FPC + f
        back = look[frame]
        k = kext[pl.ds(base, SPAN), lanes]
        v = vext[pl.ds(base, SPAN), lanes]
        q = qbuf[pl.ds(tok, CH), lanes]
        lane = lax.broadcasted_iota(jnp.int32, (CH, PAIR), 1)
        feat = lax.broadcasted_iota(jnp.int32, (PAIR, CH), 0)
        zero = jnp.zeros((CH, PAIR), BF16)
        q2 = jnp.concatenate([jnp.where(lane < HEAD, q, zero), jnp.where(lane < HEAD, zero, q)], 0)
        s = mm(k, q2 * jnp.asarray(SCALE, BF16), NT)
        parts = []
        for j in range(W + 1):
            part = s[j * CH : (j + 1) * CH]
            if j < W:
                seen = jnp.where(frame - W + j >= 0, W - j, FPC * groups)
                part = part + jnp.where(seen <= back, 0.0, -1e30)
            parts.append(part)
        s = jnp.concatenate(parts, 0)
        e = jnp.exp(s - jnp.max(s, 0, keepdims=True))
        p = e * (1.0 / jnp.sum(e, 0, keepdims=True))
        pb = p.astype(BF16)
        do = og[lanes, pl.ds(tok, CH)]
        do2 = jnp.concatenate([jnp.where(feat < HEAD, do, zero), jnp.where(feat < HEAD, zero, do)], 1)
        dp = mm(v, do2, NN)
        o2 = mm(vt[lanes, pl.ds(base, SPAN)], pb, NN)
        out = jnp.where(feat < HEAD, o2[:, :CH], o2[:, CH:]).astype(BF16)
        att[lanes, pl.ds(tok, CH)] = out
        prod = do.astype(F32) * out.astype(F32)
        inner = jnp.concatenate(
            [jnp.sum(prod[:HEAD], 0, keepdims=True), jnp.sum(prod[HEAD:], 0, keepdims=True)], 1
        )
        ds = (p * (dp - inner)).astype(BF16)
        dq2 = mm(kt[lanes, pl.ds(base, SPAN)], ds, NN)
        gq[lanes, pl.ds(tok, CH)] = (
            jnp.where(feat < HEAD, dq2[:, :CH], dq2[:, CH:]) * SCALE
        ).astype(BF16)
        acck[lanes, pl.ds(base, SPAN)] += mm(q2.T, ds, NT)
        accv[lanes, pl.ds(base, SPAN)] += mm(do2, pb, NT)

    def send_grads(hp):
        lanes = slice(hp * PAIR, hp * PAIR + PAIR)
        for g in range(2):
            gsend[0, g, lanes] = (acck[lanes, g * EXT : g * EXT + TAIL] * SCALE).astype(BF16)
            gsend[1, g, lanes] = accv[lanes, g * EXT : g * EXT + TAIL].astype(BF16)
        for a in range(2):

            @pl.when(d > 0)
            def _():
                grad_copy(a, hp, 0).start()

            @pl.when(d < last)
            def _():
                grad_copy(a, hp, 1).start()

            @pl.when(d == 0)
            def _():
                gret[a, 1, lanes] = jnp.zeros((PAIR, TAIL), BF16)

            @pl.when(d == last)
            def _():
                gret[a, 0, lanes] = gsend[a, 1, lanes]

    def finish(hp):
        lanes = slice(hp * PAIR, hp * PAIR + PAIR)
        for a in range(2):

            @pl.when(d < last)
            def _():
                grad_copy(a, hp, 0).wait_recv()

            @pl.when(d > 0)
            def _():
                grad_copy(a, hp, 1).wait_recv()

            acc, out = ((acck, gk), (accv, gv))[a]
            for g in range(2):
                own = acc[lanes, g * EXT + TAIL : (g + 1) * EXT]
                if a == 0:
                    own = own * SCALE
                own_tail = own[:, GROUP - TAIL :] + gret[a, g, lanes].astype(F32)
                out[lanes, g * GROUP : (g + 1) * GROUP - TAIL] = own[:, : GROUP - TAIL].astype(BF16)
                out[lanes, (g + 1) * GROUP - TAIL : (g + 1) * GROUP] = own_tail.astype(BF16)
            out_copy(2 + a, hp).start()

    acck[...] = jnp.zeros_like(acck)
    accv[...] = jnp.zeros_like(accv)

    def out_copy(i, hp):
        src, dst = ((att, att_out), (gq, gq_out), (gk, gk_out), (gv, gv_out))[i]
        part = pl.ds(hp * PAIR, PAIR)
        return pltpu.make_async_copy(src.at[part], dst.at[part], out_sem.at[i, hp])

    def receive(hp):
        for a in range(2):
            arrived(a, hp)
            forward_tails(a, hp)
            if a == 1 and hp + 1 < pairs:
                send(hp + 1)
            turn(a, hp, W, W + FPC)

    def items(hp, f):
        for g in range(2):
            item(hp, g, f)

    look_copy.wait()
    og_copy.wait()
    receive(0)
    for hp in range(pairs):
        arrived(2, hp)
        for a in range(2):
            tails_arrived(a, hp)
            turn(a, hp, 0, W)

        @pl.loop(0, EARLY)
        def _(f):
            items(hp, f)

        if hp + 1 < pairs:
            receive(hp + 1)

        @pl.loop(EARLY, W)
        def _(f):
            items(hp, f)

        send_grads(hp)
        items(hp, W)
        for i in range(2):
            out_copy(i, hp).start()
        if hp > 0:
            finish(hp - 1)
    finish(pairs - 1)

    for hp in range(pairs):
        for i in range(4):
            out_copy(i, hp).wait()
        for a in range(3):
            for o in range(1, tp):
                peer_copy(a, hp, o).wait_send()
        for a in range(2):

            @pl.when(d < last)
            def _():
                tail_copy(a, hp, 0).wait_send()
                grad_copy(a, hp, 1).wait_send()

            @pl.when(d > 0)
            def _():
                tail_copy(a, hp, 1).wait_send()
                grad_copy(a, hp, 0).wait_send()


def write_out(*refs):
    held, in_sem, out_sem = refs[8:]
    parts = [(i, hp) for i in range(4) for hp in range(in_sem.shape[1])]

    def load(i, hp):
        part = pl.ds(hp * PAIR, PAIR)
        return pltpu.make_async_copy(refs[i].at[part], held.at[i, part], in_sem.at[i, hp])

    def store(i, hp):
        part = pl.ds(hp * PAIR, PAIR)
        return pltpu.make_async_copy(held.at[i, part], refs[4 + i].at[part], out_sem.at[i, hp])

    for at in parts:
        load(*at).start()
    for at in parts:
        load(*at).wait()
        store(*at).start()
    for at in parts:
        store(*at).wait()


def on_device(tp, ctx, query_in, key_in, value_in, lookback, out_grad):
    feats, tokens = out_grad.shape
    pairs = feats // PAIR
    dma = pltpu.SemaphoreType.DMA
    vmem = pl.BlockSpec(memory_space=pltpu.VMEM)
    hbm = pl.BlockSpec(memory_space=pltpu.HBM)
    outs = pl.pallas_call(
        functools.partial(kernel, tp, ctx),
        out_shape=[jax.ShapeDtypeStruct((feats, tokens), BF16)] * 4,
        in_specs=[hbm] * 5,
        out_specs=[hbm] * 4,
        scratch_shapes=[
            *[pltpu.VMEM((feats, tokens), BF16) for _ in range(4)],
            pltpu.SMEM(lookback.shape, jnp.int32),
            pltpu.VMEM((feats, tokens), BF16),
            pltpu.VMEM((2 * GROUP, feats), BF16),
            pltpu.VMEM((2 * EXT, feats), BF16),
            pltpu.VMEM((2 * EXT, feats), BF16),
            pltpu.VMEM((feats, 2 * EXT), BF16),
            pltpu.VMEM((feats, 2 * EXT), BF16),
            pltpu.VMEM((feats, 2 * EXT), F32),
            pltpu.VMEM((feats, 2 * EXT), F32),
            pltpu.VMEM((2, 2, feats, TAIL), BF16),
            pltpu.VMEM((2, 2, feats, TAIL), BF16),
            dma((2,)),
            dma((4, pairs)),
            dma((3, pairs)),
            dma((3, pairs, tp - 1)),
            dma((3, pairs, tp - 1)),
            dma((2, pairs, 2)),
            dma((2, pairs, 2)),
            dma((2, pairs, 2)),
            dma((2, pairs, 2)),
        ],
        compiler_params=pltpu.CompilerParams(
            collective_id=0, has_side_effects=True, vmem_limit_bytes=61 << 20
        ),
    )(query_in, key_in, value_in, lookback, out_grad)
    return pl.pallas_call(
        write_out,
        out_shape=[jax.ShapeDtypeStruct((feats, tokens), BF16)] * 4,
        in_specs=[hbm] * 4,
        out_specs=[hbm] * 4,
        scratch_shapes=[
            pltpu.VMEM((4, feats, tokens), BF16),
            dma((4, pairs)),
            dma((4, pairs)),
        ],
        compiler_params=pltpu.CompilerParams(vmem_limit_bytes=61 << 20),
    )(*outs)


SCORE_SCALE = 0.125


def from_behind(shard, axis, by):
    length = lax.axis_size(axis)
    pairs = [(i, i + by) for i in range(length) if 0 <= i + by < length]
    return lax.ppermute(shard, axis, pairs)


def masked_scores(query_block, key_block, allowed):
    raw_scores = (
        jnp.einsum("fqhd,fkhd->fhqk", query_block, key_block, preferred_element_type=jnp.float32)
        * SCORE_SCALE
    )
    return jnp.where(allowed[:, None, None, None], raw_scores, -jnp.inf)


def stats_block(inputs, allowed):
    query_block, key_block = inputs
    masked = masked_scores(query_block, key_block, allowed)
    block_max = jnp.max(masked, -1)
    safe_max = jnp.where(block_max == -jnp.inf, 0.0, block_max)
    return (block_max, jnp.sum(jnp.exp(masked - safe_max[..., None]), -1))


def output_block(inputs, allowed):
    query_block, key_block, value_block, log_block = inputs
    weights = jnp.exp(masked_scores(query_block, key_block, allowed) - log_block[..., None]).astype(
        jnp.bfloat16
    )
    return jnp.einsum("fhqk,fkhd->fqhd", weights, value_block, preferred_element_type=jnp.float32)


def back_block(inputs, allowed):
    query_block, grad_block, log_block, inner_block, key_block, value_block = inputs
    probability = jnp.exp(masked_scores(query_block, key_block, allowed) - log_block[..., None])
    grad_prob = jnp.einsum(
        "fqhd,fkhd->fhqk", grad_block, value_block, preferred_element_type=jnp.float32
    )
    grad_score = (probability * (grad_prob - inner_block[..., None])).astype(jnp.bfloat16)
    key_part = (
        jnp.einsum("fhqk,fqhd->fkhd", grad_score, query_block, preferred_element_type=jnp.float32)
        * SCORE_SCALE
    )
    value_part = jnp.einsum(
        "fhqk,fqhd->fkhd",
        probability.astype(jnp.bfloat16),
        grad_block,
        preferred_element_type=jnp.float32,
    )
    query_part = (
        jnp.einsum("fhqk,fkhd->fqhd", grad_score, key_block, preferred_element_type=jnp.float32)
        * SCORE_SCALE
    )
    return (query_part, key_part, value_part)


def general(query_in, key_in, value_in, lookback, out_grad):
    query_rows, key_rows, value_rows = (
        lax.all_to_all(query_in, "tp", split_axis=1, concat_axis=0, tiled=True),
        lax.all_to_all(key_in, "tp", split_axis=1, concat_axis=0, tiled=True),
        lax.all_to_all(value_in, "tp", split_axis=1, concat_axis=0, tiled=True),
    )
    row_count = query_rows.shape[0]
    frame_rows = row_count // (2 * FPC)
    head_count = out_grad.shape[0] // HEAD
    ctx_count = lax.axis_size("ctx")
    group_total = 2 * ctx_count
    device = lax.axis_index("ctx")
    last_device = device == ctx_count - 1
    layout = (2, FPC, frame_rows, head_count, HEAD)
    query_heads = query_rows.reshape(layout)
    grad_heads = out_grad.T.reshape(layout)
    local_pair = jnp.stack([key_rows.reshape(layout), value_rows.reshape(layout)], 4)
    tail_width = head_count * 2 * HEAD
    low_tail = local_pair[0, FPC - W :].reshape(W * frame_rows, tail_width)
    high_tail = local_pair[1, FPC - W :].reshape(W * frame_rows, tail_width)
    below = from_behind(low_tail, "ctx", 1)
    above = from_behind(high_tail, "ctx", -1)
    above = jnp.where(last_device, low_tail, above)
    tails = jnp.stack([below, above]).reshape(2, W, frame_rows, head_count, 2, HEAD)
    extended = jnp.concatenate([tails, local_pair], 1)
    frame_ids = jnp.arange(group_total * FPC, dtype=jnp.int32)
    group_pair = jnp.stack([device, group_total - 1 - device])
    query_frame = group_pair[:, None] * FPC + jnp.arange(FPC, dtype=jnp.int32)[None, :]
    query_look = jnp.sum(jnp.where(query_frame[..., None] == frame_ids, lookback, 0), -1)
    permits = []
    for offset in range(W + 1):
        key_frame = query_frame - W + offset
        permits.append(
            ((key_frame >= 0) & (key_frame >= query_frame - query_look)).reshape(2 * FPC)
        )

    def window(offset):
        pair = extended[:, offset : offset + FPC].reshape(2 * FPC, frame_rows, head_count, 2, HEAD)
        return (pair[:, :, :, 0], pair[:, :, :, 1])

    flat_query = query_heads.reshape(2 * FPC, frame_rows, head_count, HEAD)
    flat_grad = grad_heads.reshape(2 * FPC, frame_rows, head_count, HEAD)
    block_stats = [
        stats_block((flat_query, window(offset)[0]), permits[offset]) for offset in range(W + 1)
    ]
    total_max = reduce(jnp.maximum, [entry[0] for entry in block_stats])
    total_sum = jnp.zeros_like(total_max)
    for entry in block_stats:
        total_sum = total_sum + entry[1] * jnp.exp(entry[0] - total_max)
    log_total = total_max + jnp.log(total_sum)
    summed = jnp.zeros((2 * FPC, frame_rows, head_count, HEAD), jnp.float32)
    for offset in range(W + 1):
        keys, values = window(offset)
        summed = summed + output_block((flat_query, keys, values, log_total), permits[offset])
    attention = summed.astype(jnp.bfloat16)
    inner_sum = jnp.transpose(
        jnp.sum(flat_grad.astype(jnp.float32) * attention.astype(jnp.float32), -1), (0, 2, 1)
    )

    def pad_frames(part, first, stop, length):
        shaped = part.reshape((2, stop - first) + part.shape[1:])
        return jnp.pad(shaped, ((0, 0), (first, length - stop), (0, 0), (0, 0), (0, 0)))

    grad_query = jnp.zeros((2 * FPC, frame_rows, head_count, HEAD), jnp.float32)
    key_total = jnp.zeros((2, W + FPC, frame_rows, head_count, HEAD), jnp.float32)
    value_total = jnp.zeros((2, W + FPC, frame_rows, head_count, HEAD), jnp.float32)
    for offset in range(W + 1):
        keys, values = window(offset)
        query_part, key_part, value_part = back_block(
            (flat_query, flat_grad, log_total, inner_sum, keys, values), permits[offset]
        )
        grad_query = grad_query + query_part
        key_total = key_total + pad_frames(key_part, offset, offset + FPC, W + FPC)
        value_total = value_total + pad_frames(value_part, offset, offset + FPC, W + FPC)
    tail_grads = jnp.stack([key_total[:, :W], value_total[:, :W]], 4).reshape(
        2, W * frame_rows, tail_width
    )
    from_above = from_behind(tail_grads[0].astype(jnp.bfloat16), "ctx", -1).astype(jnp.float32)
    from_below = from_behind(tail_grads[1].astype(jnp.bfloat16), "ctx", 1).astype(jnp.float32)
    returned = jnp.stack(
        [from_above + jnp.where(last_device, tail_grads[1], 0.0), from_below]
    ).reshape(2, W, frame_rows, head_count, 2, HEAD)
    tail_pad = ((0, 0), (FPC - W, 0), (0, 0), (0, 0), (0, 0))
    own_key = key_total[:, W:] + jnp.pad(returned[:, :, :, :, 0], tail_pad)
    own_value = value_total[:, W:] + jnp.pad(returned[:, :, :, :, 1], tail_pad)
    width = head_count * HEAD

    def finish(array):
        return array.astype(jnp.bfloat16).reshape(row_count, width).T

    return (
        attention.reshape(row_count, width).T,
        finish(grad_query),
        finish(own_key),
        finish(own_value),
    )


def solution(mesh):
    tp, ctx = mesh.shape["tp"], mesh.shape["ctx"]
    rows = P(("ctx", "tp"), None)
    out = P("tp", "ctx")

    def step(*args):
        if args[4].shape[0] % PAIR or args[0].shape[0] % CH:
            return general(*args)
        return on_device(tp, ctx, *args)

    return jax.shard_map(
        step,
        mesh=mesh,
        in_specs=(rows, rows, rows, P(), out),
        out_specs=(out,) * 4,
        check_vma=False,
    )
```

```python
import functools
from functools import reduce

import jax
import jax.numpy as jnp
from jax import lax
from jax.experimental import pallas as pl
from jax.experimental.pallas import tpu as pltpu
from jax.sharding import PartitionSpec as P

HEAD = 64
FPC = 4
W = 3
CH = 128
PAIR = 2 * HEAD
GROUP = FPC * CH
TAIL = W * CH
EXT = TAIL + GROUP
SPAN = (W + 1) * CH
SCALE = 0.125
EARLY = 2
MESH = pl.DeviceIdType.MESH
NT = (((1,), (1,)), ((), ()))
NN = (((1,), (0,)), ((), ()))
F32 = jnp.float32
BF16 = jnp.bfloat16


def mm(a, b, dims):
    return lax.dot_general(a, b, dims, preferred_element_type=F32)


def kernel(
    tp, ctx, q_hbm, k_hbm, v_hbm, look_hbm, og_hbm,
    att_out, gq_out, gk_out, gv_out,
    att, gq, gk, gv,
    look, og, qbuf, kext, vext, kt, vt, acck, accv, gsend, gret,
    in_sem, out_sem, own_sem, send_sem, recv_sem, tsend, trecv, gssem, grsem,
):
    rows, width = q_hbm.shape
    feats = width // tp
    pairs = feats // PAIR
    me = lax.axis_index("tp")
    d = lax.axis_index("ctx")
    last = ctx - 1
    groups = 2 * ctx

    barrier = pltpu.get_barrier_semaphore()
    for o in range(1, tp):
        pl.semaphore_signal(barrier, inc=1, device_id={"tp": lax.rem(me + o, tp)}, device_id_type=MESH)

    @pl.when(d > 0)
    def _():
        pl.semaphore_signal(barrier, inc=1, device_id={"ctx": d - 1}, device_id_type=MESH)

    @pl.when(d < last)
    def _():
        pl.semaphore_signal(barrier, inc=1, device_id={"ctx": d + 1}, device_id_type=MESH)

    def ext_row(p):
        return pl.multiple_of(p * rows + TAIL + TAIL * (p // (tp // 2)), CH)

    arrays = ((k_hbm, kext), (v_hbm, vext), (q_hbm, qbuf))

    def dst_row(a):
        return pl.multiple_of(me * rows, CH) if a == 2 else ext_row(me)

    def own_copy(a, hp):
        src, dst = arrays[a]
        return pltpu.make_async_copy(
            src.at[:, pl.ds(pl.multiple_of(me * feats + hp * PAIR, PAIR), PAIR)],
            dst.at[pl.ds(dst_row(a), rows), pl.ds(hp * PAIR, PAIR)],
            own_sem.at[a, hp],
        )

    def peer_copy(a, hp, o):
        src, dst = arrays[a]
        to = lax.rem(me + o, tp)
        return pltpu.make_async_remote_copy(
            src_ref=src.at[:, pl.ds(pl.multiple_of(to * feats + hp * PAIR, PAIR), PAIR)],
            dst_ref=dst.at[pl.ds(dst_row(a), rows), pl.ds(hp * PAIR, PAIR)],
            send_sem=send_sem.at[a, hp, o - 1],
            recv_sem=recv_sem.at[a, hp, o - 1],
            device_id={"tp": to},
            device_id_type=MESH,
        )

    look_copy = pltpu.make_async_copy(look_hbm, look, in_sem.at[0])
    og_copy = pltpu.make_async_copy(og_hbm, og, in_sem.at[1])
    amount = tp - 1 + jnp.where(d > 0, 1, 0) + jnp.where(d < last, 1, 0)
    pl.semaphore_wait(barrier, amount)

    def send(hp):
        for a in range(3):
            for o in range(1, tp):
                peer_copy(a, hp, o).start()

    send(0)
    for hp in range(pairs):
        for a in range(3):
            own_copy(a, hp).start()
    look_copy.start()
    og_copy.start()

    def arrived(a, hp):
        own_copy(a, hp).wait()
        for o in range(1, tp):
            peer_copy(a, hp, o).wait_recv()

    def tail_copy(a, hp, g):
        buf = arrays[a][1]
        return pltpu.make_async_remote_copy(
            src_ref=buf.at[pl.ds(g * EXT + EXT - TAIL, TAIL), pl.ds(hp * PAIR, PAIR)],
            dst_ref=buf.at[pl.ds(g * EXT, TAIL), pl.ds(hp * PAIR, PAIR)],
            send_sem=tsend.at[a, hp, g],
            recv_sem=trecv.at[a, hp, g],
            device_id={"ctx": d + 1 - 2 * g},
            device_id_type=MESH,
        )

    def grad_copy(a, hp, g):
        return pltpu.make_async_remote_copy(
            src_ref=gsend.at[a, g, pl.ds(hp * PAIR, PAIR)],
            dst_ref=gret.at[a, g, pl.ds(hp * PAIR, PAIR)],
            send_sem=gssem.at[a, hp, g],
            recv_sem=grsem.at[a, hp, g],
            device_id={"ctx": d - 1 + 2 * g},
            device_id_type=MESH,
        )

    def forward_tails(a, hp):
        lanes = slice(hp * PAIR, hp * PAIR + PAIR)
        buf = arrays[a][1]

        @pl.when(d < last)
        def _():
            tail_copy(a, hp, 0).start()

        @pl.when(d > 0)
        def _():
            tail_copy(a, hp, 1).start()

        @pl.when(d == 0)
        def _():
            buf[0:TAIL, lanes] = jnp.zeros((TAIL, PAIR), BF16)

        @pl.when(d == last)
        def _():
            buf[EXT : EXT + TAIL, lanes] = buf[EXT - TAIL : EXT, lanes]

    def tails_arrived(a, hp):
        @pl.when(d > 0)
        def _():
            tail_copy(a, hp, 0).wait_recv()

        @pl.when(d < last)
        def _():
            tail_copy(a, hp, 1).wait_recv()

    def turn(a, hp, first, stop):
        buf, out = ((kext, kt), (vext, vt))[a]
        lanes = slice(hp * PAIR, hp * PAIR + PAIR)
        for g in range(2):
            at = slice(g * EXT + first * CH, g * EXT + stop * CH)
            out[lanes, at] = buf[at, lanes].T

    def item(hp, g, f):
        lanes = slice(hp * PAIR, hp * PAIR + PAIR)
        base = pl.multiple_of(g * EXT + f * CH, CH)
        tok = pl.multiple_of(g * GROUP + f * CH, CH)
        frame = jnp.where(g == 0, d, groups - 1 - d) * FPC + f
        back = look[frame]
        k = kext[pl.ds(base, SPAN), lanes]
        v = vext[pl.ds(base, SPAN), lanes]
        q = qbuf[pl.ds(tok, CH), lanes]
        lane = lax.broadcasted_iota(jnp.int32, (CH, PAIR), 1)
        feat = lax.broadcasted_iota(jnp.int32, (PAIR, CH), 0)
        zero = jnp.zeros((CH, PAIR), BF16)
        q2 = jnp.concatenate([jnp.where(lane < HEAD, q, zero), jnp.where(lane < HEAD, zero, q)], 0)
        s = mm(k, q2 * jnp.asarray(SCALE, BF16), NT)
        yield
        parts = []
        for j in range(W + 1):
            part = s[j * CH : (j + 1) * CH]
            if j < W:
                seen = jnp.where(frame - W + j >= 0, W - j, FPC * groups)
                part = part + jnp.where(seen <= back, 0.0, -1e30)
            parts.append(part)
        s = jnp.concatenate(parts, 0)
        e = jnp.exp(s - jnp.max(s, 0, keepdims=True))
        p = e * (1.0 / jnp.sum(e, 0, keepdims=True))
        pb = p.astype(BF16)
        yield
        do = og[lanes, pl.ds(tok, CH)]
        do2 = jnp.concatenate([jnp.where(feat < HEAD, do, zero), jnp.where(feat < HEAD, zero, do)], 1)
        dp = mm(v, do2, NN)
        o2 = mm(vt[lanes, pl.ds(base, SPAN)], pb, NN)
        out = jnp.where(feat < HEAD, o2[:, :CH], o2[:, CH:]).astype(BF16)
        att[lanes, pl.ds(tok, CH)] = out
        prod = do.astype(F32) * out.astype(F32)
        inner = jnp.concatenate(
            [jnp.sum(prod[:HEAD], 0, keepdims=True), jnp.sum(prod[HEAD:], 0, keepdims=True)], 1
        )
        yield
        ds = (p * (dp - inner)).astype(BF16)
        yield
        dq2 = mm(kt[lanes, pl.ds(base, SPAN)], ds, NN)
        gq[lanes, pl.ds(tok, CH)] = (
            jnp.where(feat < HEAD, dq2[:, :CH], dq2[:, CH:]) * SCALE
        ).astype(BF16)
        acck[lanes, pl.ds(base, SPAN)] += mm(q2.T, ds, NT)
        accv[lanes, pl.ds(base, SPAN)] += mm(do2, pb, NT)

    def send_grads(hp):
        lanes = slice(hp * PAIR, hp * PAIR + PAIR)
        for g in range(2):
            gsend[0, g, lanes] = (acck[lanes, g * EXT : g * EXT + TAIL] * SCALE).astype(BF16)
            gsend[1, g, lanes] = accv[lanes, g * EXT : g * EXT + TAIL].astype(BF16)
        for a in range(2):

            @pl.when(d > 0)
            def _():
                grad_copy(a, hp, 0).start()

            @pl.when(d < last)
            def _():
                grad_copy(a, hp, 1).start()

            @pl.when(d == 0)
            def _():
                gret[a, 1, lanes] = jnp.zeros((PAIR, TAIL), BF16)

            @pl.when(d == last)
            def _():
                gret[a, 0, lanes] = gsend[a, 1, lanes]

    def finish(hp):
        lanes = slice(hp * PAIR, hp * PAIR + PAIR)
        for a in range(2):

            @pl.when(d < last)
            def _():
                grad_copy(a, hp, 0).wait_recv()

            @pl.when(d > 0)
            def _():
                grad_copy(a, hp, 1).wait_recv()

            acc, out = ((acck, gk), (accv, gv))[a]
            for g in range(2):
                own = acc[lanes, g * EXT + TAIL : (g + 1) * EXT]
                if a == 0:
                    own = own * SCALE
                own_tail = own[:, GROUP - TAIL :] + gret[a, g, lanes].astype(F32)
                out[lanes, g * GROUP : (g + 1) * GROUP - TAIL] = own[:, : GROUP - TAIL].astype(BF16)
                out[lanes, (g + 1) * GROUP - TAIL : (g + 1) * GROUP] = own_tail.astype(BF16)
            out_copy(2 + a, hp).start()

    acck[...] = jnp.zeros_like(acck)
    accv[...] = jnp.zeros_like(accv)

    def out_copy(i, hp):
        src, dst = ((att, att_out), (gq, gq_out), (gk, gk_out), (gv, gv_out))[i]
        part = pl.ds(hp * PAIR, PAIR)
        return pltpu.make_async_copy(src.at[part], dst.at[part], out_sem.at[i, hp])

    def receive(hp):
        for a in range(2):
            arrived(a, hp)
            forward_tails(a, hp)
            if a == 1 and hp + 1 < pairs:
                send(hp + 1)
            turn(a, hp, W, W + FPC)

    def items(hp, f):
        steps = [item(hp, g, f) for g in range(2)]
        for _ in range(5):
            for step in steps:
                next(step, None)

    look_copy.wait()
    og_copy.wait()
    receive(0)
    for hp in range(pairs):
        arrived(2, hp)
        if hp + 1 < pairs:
            items(hp, W)
        for a in range(2):
            tails_arrived(a, hp)
            turn(a, hp, 0, W)

        @pl.loop(0, EARLY)
        def _(f):
            items(hp, f)

        if hp + 1 < pairs:
            receive(hp + 1)

        @pl.loop(EARLY, W)
        def _(f):
            items(hp, f)

        send_grads(hp)
        if hp + 1 == pairs:
            items(hp, W)
        for i in range(2):
            out_copy(i, hp).start()
        if hp > 0:
            finish(hp - 1)
    finish(pairs - 1)

    for hp in range(pairs):
        for i in range(4):
            out_copy(i, hp).wait()
        for a in range(3):
            for o in range(1, tp):
                peer_copy(a, hp, o).wait_send()
        for a in range(2):

            @pl.when(d < last)
            def _():
                tail_copy(a, hp, 0).wait_send()
                grad_copy(a, hp, 1).wait_send()

            @pl.when(d > 0)
            def _():
                tail_copy(a, hp, 1).wait_send()
                grad_copy(a, hp, 0).wait_send()


def write_out(*refs):
    held, in_sem, out_sem = refs[8:]
    parts = [(i, hp) for i in range(4) for hp in range(in_sem.shape[1])]

    def load(i, hp):
        part = pl.ds(hp * PAIR, PAIR)
        return pltpu.make_async_copy(refs[i].at[part], held.at[i, part], in_sem.at[i, hp])

    def store(i, hp):
        part = pl.ds(hp * PAIR, PAIR)
        return pltpu.make_async_copy(held.at[i, part], refs[4 + i].at[part], out_sem.at[i, hp])

    for at in parts:
        load(*at).start()
    for at in parts:
        load(*at).wait()
        store(*at).start()
    for at in parts:
        store(*at).wait()


def on_device(tp, ctx, query_in, key_in, value_in, lookback, out_grad):
    feats, tokens = out_grad.shape
    pairs = feats // PAIR
    dma = pltpu.SemaphoreType.DMA
    vmem = pl.BlockSpec(memory_space=pltpu.VMEM)
    hbm = pl.BlockSpec(memory_space=pltpu.HBM)
    outs = pl.pallas_call(
        functools.partial(kernel, tp, ctx),
        out_shape=[jax.ShapeDtypeStruct((feats, tokens), BF16)] * 4,
        in_specs=[hbm] * 5,
        out_specs=[hbm] * 4,
        scratch_shapes=[
            *[pltpu.VMEM((feats, tokens), BF16) for _ in range(4)],
            pltpu.SMEM(lookback.shape, jnp.int32),
            pltpu.VMEM((feats, tokens), BF16),
            pltpu.VMEM((2 * GROUP, feats), BF16),
            pltpu.VMEM((2 * EXT, feats), BF16),
            pltpu.VMEM((2 * EXT, feats), BF16),
            pltpu.VMEM((feats, 2 * EXT), BF16),
            pltpu.VMEM((feats, 2 * EXT), BF16),
            pltpu.VMEM((feats, 2 * EXT), F32),
            pltpu.VMEM((feats, 2 * EXT), F32),
            pltpu.VMEM((2, 2, feats, TAIL), BF16),
            pltpu.VMEM((2, 2, feats, TAIL), BF16),
            dma((2,)),
            dma((4, pairs)),
            dma((3, pairs)),
            dma((3, pairs, tp - 1)),
            dma((3, pairs, tp - 1)),
            dma((2, pairs, 2)),
            dma((2, pairs, 2)),
            dma((2, pairs, 2)),
            dma((2, pairs, 2)),
        ],
        compiler_params=pltpu.CompilerParams(
            collective_id=0, has_side_effects=True, vmem_limit_bytes=61 << 20
        ),
    )(query_in, key_in, value_in, lookback, out_grad)
    return pl.pallas_call(
        write_out,
        out_shape=[jax.ShapeDtypeStruct((feats, tokens), BF16)] * 4,
        in_specs=[hbm] * 4,
        out_specs=[hbm] * 4,
        scratch_shapes=[
            pltpu.VMEM((4, feats, tokens), BF16),
            dma((4, pairs)),
            dma((4, pairs)),
        ],
        compiler_params=pltpu.CompilerParams(vmem_limit_bytes=61 << 20),
    )(*outs)


SCORE_SCALE = 0.125


def from_behind(shard, axis, by):
    length = lax.axis_size(axis)
    pairs = [(i, i + by) for i in range(length) if 0 <= i + by < length]
    return lax.ppermute(shard, axis, pairs)


def masked_scores(query_block, key_block, allowed):
    raw_scores = (
        jnp.einsum("fqhd,fkhd->fhqk", query_block, key_block, preferred_element_type=jnp.float32)
        * SCORE_SCALE
    )
    return jnp.where(allowed[:, None, None, None], raw_scores, -jnp.inf)


def stats_block(inputs, allowed):
    query_block, key_block = inputs
    masked = masked_scores(query_block, key_block, allowed)
    block_max = jnp.max(masked, -1)
    safe_max = jnp.where(block_max == -jnp.inf, 0.0, block_max)
    return (block_max, jnp.sum(jnp.exp(masked - safe_max[..., None]), -1))


def output_block(inputs, allowed):
    query_block, key_block, value_block, log_block = inputs
    weights = jnp.exp(masked_scores(query_block, key_block, allowed) - log_block[..., None]).astype(
        jnp.bfloat16
    )
    return jnp.einsum("fhqk,fkhd->fqhd", weights, value_block, preferred_element_type=jnp.float32)


def back_block(inputs, allowed):
    query_block, grad_block, log_block, inner_block, key_block, value_block = inputs
    probability = jnp.exp(masked_scores(query_block, key_block, allowed) - log_block[..., None])
    grad_prob = jnp.einsum(
        "fqhd,fkhd->fhqk", grad_block, value_block, preferred_element_type=jnp.float32
    )
    grad_score = (probability * (grad_prob - inner_block[..., None])).astype(jnp.bfloat16)
    key_part = (
        jnp.einsum("fhqk,fqhd->fkhd", grad_score, query_block, preferred_element_type=jnp.float32)
        * SCORE_SCALE
    )
    value_part = jnp.einsum(
        "fhqk,fqhd->fkhd",
        probability.astype(jnp.bfloat16),
        grad_block,
        preferred_element_type=jnp.float32,
    )
    query_part = (
        jnp.einsum("fhqk,fkhd->fqhd", grad_score, key_block, preferred_element_type=jnp.float32)
        * SCORE_SCALE
    )
    return (query_part, key_part, value_part)


def general(query_in, key_in, value_in, lookback, out_grad):
    query_rows, key_rows, value_rows = (
        lax.all_to_all(query_in, "tp", split_axis=1, concat_axis=0, tiled=True),
        lax.all_to_all(key_in, "tp", split_axis=1, concat_axis=0, tiled=True),
        lax.all_to_all(value_in, "tp", split_axis=1, concat_axis=0, tiled=True),
    )
    row_count = query_rows.shape[0]
    frame_rows = row_count // (2 * FPC)
    head_count = out_grad.shape[0] // HEAD
    ctx_count = lax.axis_size("ctx")
    group_total = 2 * ctx_count
    device = lax.axis_index("ctx")
    last_device = device == ctx_count - 1
    layout = (2, FPC, frame_rows, head_count, HEAD)
    query_heads = query_rows.reshape(layout)
    grad_heads = out_grad.T.reshape(layout)
    local_pair = jnp.stack([key_rows.reshape(layout), value_rows.reshape(layout)], 4)
    tail_width = head_count * 2 * HEAD
    low_tail = local_pair[0, FPC - W :].reshape(W * frame_rows, tail_width)
    high_tail = local_pair[1, FPC - W :].reshape(W * frame_rows, tail_width)
    below = from_behind(low_tail, "ctx", 1)
    above = from_behind(high_tail, "ctx", -1)
    above = jnp.where(last_device, low_tail, above)
    tails = jnp.stack([below, above]).reshape(2, W, frame_rows, head_count, 2, HEAD)
    extended = jnp.concatenate([tails, local_pair], 1)
    frame_ids = jnp.arange(group_total * FPC, dtype=jnp.int32)
    group_pair = jnp.stack([device, group_total - 1 - device])
    query_frame = group_pair[:, None] * FPC + jnp.arange(FPC, dtype=jnp.int32)[None, :]
    query_look = jnp.sum(jnp.where(query_frame[..., None] == frame_ids, lookback, 0), -1)
    permits = []
    for offset in range(W + 1):
        key_frame = query_frame - W + offset
        permits.append(
            ((key_frame >= 0) & (key_frame >= query_frame - query_look)).reshape(2 * FPC)
        )

    def window(offset):
        pair = extended[:, offset : offset + FPC].reshape(2 * FPC, frame_rows, head_count, 2, HEAD)
        return (pair[:, :, :, 0], pair[:, :, :, 1])

    flat_query = query_heads.reshape(2 * FPC, frame_rows, head_count, HEAD)
    flat_grad = grad_heads.reshape(2 * FPC, frame_rows, head_count, HEAD)
    block_stats = [
        stats_block((flat_query, window(offset)[0]), permits[offset]) for offset in range(W + 1)
    ]
    total_max = reduce(jnp.maximum, [entry[0] for entry in block_stats])
    total_sum = jnp.zeros_like(total_max)
    for entry in block_stats:
        total_sum = total_sum + entry[1] * jnp.exp(entry[0] - total_max)
    log_total = total_max + jnp.log(total_sum)
    summed = jnp.zeros((2 * FPC, frame_rows, head_count, HEAD), jnp.float32)
    for offset in range(W + 1):
        keys, values = window(offset)
        summed = summed + output_block((flat_query, keys, values, log_total), permits[offset])
    attention = summed.astype(jnp.bfloat16)
    inner_sum = jnp.transpose(
        jnp.sum(flat_grad.astype(jnp.float32) * attention.astype(jnp.float32), -1), (0, 2, 1)
    )

    def pad_frames(part, first, stop, length):
        shaped = part.reshape((2, stop - first) + part.shape[1:])
        return jnp.pad(shaped, ((0, 0), (first, length - stop), (0, 0), (0, 0), (0, 0)))

    grad_query = jnp.zeros((2 * FPC, frame_rows, head_count, HEAD), jnp.float32)
    key_total = jnp.zeros((2, W + FPC, frame_rows, head_count, HEAD), jnp.float32)
    value_total = jnp.zeros((2, W + FPC, frame_rows, head_count, HEAD), jnp.float32)
    for offset in range(W + 1):
        keys, values = window(offset)
        query_part, key_part, value_part = back_block(
            (flat_query, flat_grad, log_total, inner_sum, keys, values), permits[offset]
        )
        grad_query = grad_query + query_part
        key_total = key_total + pad_frames(key_part, offset, offset + FPC, W + FPC)
        value_total = value_total + pad_frames(value_part, offset, offset + FPC, W + FPC)
    tail_grads = jnp.stack([key_total[:, :W], value_total[:, :W]], 4).reshape(
        2, W * frame_rows, tail_width
    )
    from_above = from_behind(tail_grads[0].astype(jnp.bfloat16), "ctx", -1).astype(jnp.float32)
    from_below = from_behind(tail_grads[1].astype(jnp.bfloat16), "ctx", 1).astype(jnp.float32)
    returned = jnp.stack(
        [from_above + jnp.where(last_device, tail_grads[1], 0.0), from_below]
    ).reshape(2, W, frame_rows, head_count, 2, HEAD)
    tail_pad = ((0, 0), (FPC - W, 0), (0, 0), (0, 0), (0, 0))
    own_key = key_total[:, W:] + jnp.pad(returned[:, :, :, :, 0], tail_pad)
    own_value = value_total[:, W:] + jnp.pad(returned[:, :, :, :, 1], tail_pad)
    width = head_count * HEAD

    def finish(array):
        return array.astype(jnp.bfloat16).reshape(row_count, width).T

    return (
        attention.reshape(row_count, width).T,
        finish(grad_query),
        finish(own_key),
        finish(own_value),
    )


def solution(mesh):
    tp, ctx = mesh.shape["tp"], mesh.shape["ctx"]
    rows = P(("ctx", "tp"), None)
    out = P("tp", "ctx")

    def step(*args):
        if args[4].shape[0] % PAIR or args[0].shape[0] % CH:
            return general(*args)
        return on_device(tp, ctx, *args)

    return jax.shard_map(
        step,
        mesh=mesh,
        in_specs=(rows, rows, rows, P(), out),
        out_specs=(out,) * 4,
        check_vma=False,
    )
```

```python
import functools
from functools import reduce

import jax
import jax.numpy as jnp
from jax import lax
from jax.experimental import pallas as pl
from jax.experimental.pallas import tpu as pltpu
from jax.sharding import PartitionSpec as P

HEAD = 64
FPC = 4
W = 3
CH = 128
PAIR = 2 * HEAD
GROUP = FPC * CH
TAIL = W * CH
EXT = TAIL + GROUP
SPAN = (W + 1) * CH
SCALE = 0.125
EARLY = 2
MESH = pl.DeviceIdType.MESH
NT = (((1,), (1,)), ((), ()))
NN = (((1,), (0,)), ((), ()))
F32 = jnp.float32
BF16 = jnp.bfloat16


def mm(a, b, dims):
    return lax.dot_general(a, b, dims, preferred_element_type=F32)


def kernel(
    tp, ctx, q_hbm, k_hbm, v_hbm, look_hbm, og_hbm,
    att_out, gq_out, gk_out, gv_out,
    att, gq, gk, gv,
    look, og, qbuf, kext, vext, kt, vt, acck, accv, gsend, gret,
    in_sem, out_sem, own_sem, send_sem, recv_sem, tsend, trecv, gssem, grsem,
):
    rows, width = q_hbm.shape
    feats = width // tp
    pairs = feats // PAIR
    me = lax.axis_index("tp")
    d = lax.axis_index("ctx")
    last = ctx - 1
    groups = 2 * ctx

    barrier = pltpu.get_barrier_semaphore()
    for o in range(1, tp):
        pl.semaphore_signal(barrier, inc=1, device_id={"tp": lax.rem(me + o, tp)}, device_id_type=MESH)

    @pl.when(d > 0)
    def _():
        pl.semaphore_signal(barrier, inc=1, device_id={"ctx": d - 1}, device_id_type=MESH)

    @pl.when(d < last)
    def _():
        pl.semaphore_signal(barrier, inc=1, device_id={"ctx": d + 1}, device_id_type=MESH)

    def ext_row(p):
        return pl.multiple_of(p * rows + TAIL + TAIL * (p // (tp // 2)), CH)

    arrays = ((k_hbm, kext), (v_hbm, vext), (q_hbm, qbuf))

    def dst_row(a):
        return pl.multiple_of(me * rows, CH) if a == 2 else ext_row(me)

    def own_copy(a, hp):
        src, dst = arrays[a]
        return pltpu.make_async_copy(
            src.at[:, pl.ds(pl.multiple_of(me * feats + hp * PAIR, PAIR), PAIR)],
            dst.at[pl.ds(dst_row(a), rows), pl.ds(hp * PAIR, PAIR)],
            own_sem.at[a, hp],
        )

    def peer_copy(a, hp, o):
        src, dst = arrays[a]
        to = lax.rem(me + o, tp)
        return pltpu.make_async_remote_copy(
            src_ref=src.at[:, pl.ds(pl.multiple_of(to * feats + hp * PAIR, PAIR), PAIR)],
            dst_ref=dst.at[pl.ds(dst_row(a), rows), pl.ds(hp * PAIR, PAIR)],
            send_sem=send_sem.at[a, hp, o - 1],
            recv_sem=recv_sem.at[a, hp, o - 1],
            device_id={"tp": to},
            device_id_type=MESH,
        )

    look_copy = pltpu.make_async_copy(look_hbm, look, in_sem.at[0])
    og_copy = pltpu.make_async_copy(og_hbm, og, in_sem.at[1])
    amount = tp - 1 + jnp.where(d > 0, 1, 0) + jnp.where(d < last, 1, 0)
    pl.semaphore_wait(barrier, amount)

    def send(hp):
        for a in range(3):
            for o in range(1, tp):
                peer_copy(a, hp, o).start()

    send(0)
    for hp in range(pairs):
        for a in range(3):
            own_copy(a, hp).start()
    look_copy.start()
    og_copy.start()

    def arrived(a, hp):
        own_copy(a, hp).wait()
        for o in range(1, tp):
            peer_copy(a, hp, o).wait_recv()

    def tail_copy(a, hp, g):
        buf = arrays[a][1]
        return pltpu.make_async_remote_copy(
            src_ref=buf.at[pl.ds(g * EXT + EXT - TAIL, TAIL), pl.ds(hp * PAIR, PAIR)],
            dst_ref=buf.at[pl.ds(g * EXT, TAIL), pl.ds(hp * PAIR, PAIR)],
            send_sem=tsend.at[a, hp, g],
            recv_sem=trecv.at[a, hp, g],
            device_id={"ctx": d + 1 - 2 * g},
            device_id_type=MESH,
        )

    def grad_copy(a, hp, g):
        return pltpu.make_async_remote_copy(
            src_ref=gsend.at[a, g, pl.ds(hp * PAIR, PAIR)],
            dst_ref=gret.at[a, g, pl.ds(hp * PAIR, PAIR)],
            send_sem=gssem.at[a, hp, g],
            recv_sem=grsem.at[a, hp, g],
            device_id={"ctx": d - 1 + 2 * g},
            device_id_type=MESH,
        )

    def forward_tails(a, hp):
        lanes = slice(hp * PAIR, hp * PAIR + PAIR)
        buf = arrays[a][1]

        @pl.when(d < last)
        def _():
            tail_copy(a, hp, 0).start()

        @pl.when(d > 0)
        def _():
            tail_copy(a, hp, 1).start()

        @pl.when(d == 0)
        def _():
            buf[0:TAIL, lanes] = jnp.zeros((TAIL, PAIR), BF16)

        @pl.when(d == last)
        def _():
            buf[EXT : EXT + TAIL, lanes] = buf[EXT - TAIL : EXT, lanes]

    def tails_arrived(a, hp):
        @pl.when(d > 0)
        def _():
            tail_copy(a, hp, 0).wait_recv()

        @pl.when(d < last)
        def _():
            tail_copy(a, hp, 1).wait_recv()

    def turn(a, hp, first, stop):
        buf, out = ((kext, kt), (vext, vt))[a]
        lanes = slice(hp * PAIR, hp * PAIR + PAIR)
        for g in range(2):
            at = slice(g * EXT + first * CH, g * EXT + stop * CH)
            out[lanes, at] = buf[at, lanes].T

    def item(hp, g, f):
        lanes = slice(hp * PAIR, hp * PAIR + PAIR)
        base = pl.multiple_of(g * EXT + f * CH, CH)
        tok = pl.multiple_of(g * GROUP + f * CH, CH)
        frame = jnp.where(g == 0, d, groups - 1 - d) * FPC + f
        back = look[frame]
        k = kext[pl.ds(base, SPAN), lanes]
        v = vext[pl.ds(base, SPAN), lanes]
        q = qbuf[pl.ds(tok, CH), lanes]
        lane = lax.broadcasted_iota(jnp.int32, (CH, PAIR), 1)
        feat = lax.broadcasted_iota(jnp.int32, (PAIR, CH), 0)
        zero = jnp.zeros((CH, PAIR), BF16)
        q2 = jnp.concatenate([jnp.where(lane < HEAD, q, zero), jnp.where(lane < HEAD, zero, q)], 0)
        s = mm(k, q2 * jnp.asarray(SCALE, BF16), NT)
        yield
        parts = []
        for j in range(W + 1):
            part = s[j * CH : (j + 1) * CH]
            if j < W:
                seen = jnp.where(frame - W + j >= 0, W - j, FPC * groups)
                part = part + jnp.where(seen <= back, 0.0, -1e30)
            parts.append(part)
        s = jnp.concatenate(parts, 0)
        e = jnp.exp(s - jnp.max(s, 0, keepdims=True))
        p = e * (1.0 / jnp.sum(e, 0, keepdims=True))
        pb = p.astype(BF16)
        yield
        do = og[lanes, pl.ds(tok, CH)]
        do2 = jnp.concatenate([jnp.where(feat < HEAD, do, zero), jnp.where(feat < HEAD, zero, do)], 1)
        dp = mm(v, do2, NN)
        o2 = mm(vt[lanes, pl.ds(base, SPAN)], pb, NN)
        out = jnp.where(feat < HEAD, o2[:, :CH], o2[:, CH:]).astype(BF16)
        att[lanes, pl.ds(tok, CH)] = out
        prod = do.astype(F32) * out.astype(F32)
        inner = jnp.concatenate(
            [jnp.sum(prod[:HEAD], 0, keepdims=True), jnp.sum(prod[HEAD:], 0, keepdims=True)], 1
        )
        yield
        ds = (p * (dp - inner)).astype(BF16)
        yield
        dq2 = mm(kt[lanes, pl.ds(base, SPAN)], ds, NN)
        gq[lanes, pl.ds(tok, CH)] = (
            jnp.where(feat < HEAD, dq2[:, :CH], dq2[:, CH:]) * SCALE
        ).astype(BF16)
        acck[lanes, pl.ds(base, SPAN)] += mm(q2.T, ds, NT)
        accv[lanes, pl.ds(base, SPAN)] += mm(do2, pb, NT)

    def send_grads(hp):
        lanes = slice(hp * PAIR, hp * PAIR + PAIR)
        for g in range(2):
            gsend[0, g, lanes] = (acck[lanes, g * EXT : g * EXT + TAIL] * SCALE).astype(BF16)
            gsend[1, g, lanes] = accv[lanes, g * EXT : g * EXT + TAIL].astype(BF16)
        for a in range(2):

            @pl.when(d > 0)
            def _():
                grad_copy(a, hp, 0).start()

            @pl.when(d < last)
            def _():
                grad_copy(a, hp, 1).start()

            @pl.when(d == 0)
            def _():
                gret[a, 1, lanes] = jnp.zeros((PAIR, TAIL), BF16)

            @pl.when(d == last)
            def _():
                gret[a, 0, lanes] = gsend[a, 1, lanes]

    def finish(hp):
        lanes = slice(hp * PAIR, hp * PAIR + PAIR)
        for a in range(2):

            @pl.when(d < last)
            def _():
                grad_copy(a, hp, 0).wait_recv()

            @pl.when(d > 0)
            def _():
                grad_copy(a, hp, 1).wait_recv()

            acc, out = ((acck, gk), (accv, gv))[a]
            for g in range(2):
                own = acc[lanes, g * EXT + TAIL : (g + 1) * EXT]
                if a == 0:
                    own = own * SCALE
                own_tail = own[:, GROUP - TAIL :] + gret[a, g, lanes].astype(F32)
                out[lanes, g * GROUP : (g + 1) * GROUP - TAIL] = own[:, : GROUP - TAIL].astype(BF16)
                out[lanes, (g + 1) * GROUP - TAIL : (g + 1) * GROUP] = own_tail.astype(BF16)
            out_copy(2 + a, hp).start()

    acck[...] = jnp.zeros_like(acck)
    accv[...] = jnp.zeros_like(accv)

    def out_copy(i, hp):
        src, dst = ((att, att_out), (gq, gq_out), (gk, gk_out), (gv, gv_out))[i]
        part = pl.ds(hp * PAIR, PAIR)
        return pltpu.make_async_copy(src.at[part], dst.at[part], out_sem.at[i, hp])

    def receive(hp):
        for a in range(2):
            arrived(a, hp)
            forward_tails(a, hp)
            if a == 1 and hp + 1 < pairs:
                send(hp + 1)
            turn(a, hp, W, W + FPC)

    def items(hp, f):
        steps = [item(hp, g, f) for g in range(2)]
        for _ in range(5):
            for step in steps:
                next(step, None)

    look_copy.wait()
    og_copy.wait()
    receive(0)
    for hp in range(pairs):
        arrived(2, hp)
        if hp + 1 < pairs:
            items(hp, W)
        for a in range(2):
            tails_arrived(a, hp)
            turn(a, hp, 0, W)

        for f in range(EARLY):
            items(hp, f)

        if hp + 1 < pairs:
            receive(hp + 1)

        for f in range(EARLY, W):
            items(hp, f)

        send_grads(hp)
        if hp + 1 == pairs:
            items(hp, W)
        for i in range(2):
            out_copy(i, hp).start()
        if hp > 0:
            finish(hp - 1)
    finish(pairs - 1)

    for hp in range(pairs):
        for i in range(4):
            out_copy(i, hp).wait()
        for a in range(3):
            for o in range(1, tp):
                peer_copy(a, hp, o).wait_send()
        for a in range(2):

            @pl.when(d < last)
            def _():
                tail_copy(a, hp, 0).wait_send()
                grad_copy(a, hp, 1).wait_send()

            @pl.when(d > 0)
            def _():
                tail_copy(a, hp, 1).wait_send()
                grad_copy(a, hp, 0).wait_send()


def write_out(*refs):
    held, in_sem, out_sem = refs[8:]
    parts = [(i, hp) for i in range(4) for hp in range(in_sem.shape[1])]

    def load(i, hp):
        part = pl.ds(hp * PAIR, PAIR)
        return pltpu.make_async_copy(refs[i].at[part], held.at[i, part], in_sem.at[i, hp])

    def store(i, hp):
        part = pl.ds(hp * PAIR, PAIR)
        return pltpu.make_async_copy(held.at[i, part], refs[4 + i].at[part], out_sem.at[i, hp])

    for at in parts:
        load(*at).start()
    for at in parts:
        load(*at).wait()
        store(*at).start()
    for at in parts:
        store(*at).wait()


def on_device(tp, ctx, query_in, key_in, value_in, lookback, out_grad):
    feats, tokens = out_grad.shape
    pairs = feats // PAIR
    dma = pltpu.SemaphoreType.DMA
    vmem = pl.BlockSpec(memory_space=pltpu.VMEM)
    hbm = pl.BlockSpec(memory_space=pltpu.HBM)
    outs = pl.pallas_call(
        functools.partial(kernel, tp, ctx),
        out_shape=[jax.ShapeDtypeStruct((feats, tokens), BF16)] * 4,
        in_specs=[hbm] * 5,
        out_specs=[hbm] * 4,
        scratch_shapes=[
            *[pltpu.VMEM((feats, tokens), BF16) for _ in range(4)],
            pltpu.SMEM(lookback.shape, jnp.int32),
            pltpu.VMEM((feats, tokens), BF16),
            pltpu.VMEM((2 * GROUP, feats), BF16),
            pltpu.VMEM((2 * EXT, feats), BF16),
            pltpu.VMEM((2 * EXT, feats), BF16),
            pltpu.VMEM((feats, 2 * EXT), BF16),
            pltpu.VMEM((feats, 2 * EXT), BF16),
            pltpu.VMEM((feats, 2 * EXT), F32),
            pltpu.VMEM((feats, 2 * EXT), F32),
            pltpu.VMEM((2, 2, feats, TAIL), BF16),
            pltpu.VMEM((2, 2, feats, TAIL), BF16),
            dma((2,)),
            dma((4, pairs)),
            dma((3, pairs)),
            dma((3, pairs, tp - 1)),
            dma((3, pairs, tp - 1)),
            dma((2, pairs, 2)),
            dma((2, pairs, 2)),
            dma((2, pairs, 2)),
            dma((2, pairs, 2)),
        ],
        compiler_params=pltpu.CompilerParams(
            collective_id=0, has_side_effects=True, vmem_limit_bytes=61 << 20
        ),
    )(query_in, key_in, value_in, lookback, out_grad)
    return pl.pallas_call(
        write_out,
        out_shape=[jax.ShapeDtypeStruct((feats, tokens), BF16)] * 4,
        in_specs=[hbm] * 4,
        out_specs=[hbm] * 4,
        scratch_shapes=[
            pltpu.VMEM((4, feats, tokens), BF16),
            dma((4, pairs)),
            dma((4, pairs)),
        ],
        compiler_params=pltpu.CompilerParams(vmem_limit_bytes=61 << 20),
    )(*outs)


SCORE_SCALE = 0.125


def from_behind(shard, axis, by):
    length = lax.axis_size(axis)
    pairs = [(i, i + by) for i in range(length) if 0 <= i + by < length]
    return lax.ppermute(shard, axis, pairs)


def masked_scores(query_block, key_block, allowed):
    raw_scores = (
        jnp.einsum("fqhd,fkhd->fhqk", query_block, key_block, preferred_element_type=jnp.float32)
        * SCORE_SCALE
    )
    return jnp.where(allowed[:, None, None, None], raw_scores, -jnp.inf)


def stats_block(inputs, allowed):
    query_block, key_block = inputs
    masked = masked_scores(query_block, key_block, allowed)
    block_max = jnp.max(masked, -1)
    safe_max = jnp.where(block_max == -jnp.inf, 0.0, block_max)
    return (block_max, jnp.sum(jnp.exp(masked - safe_max[..., None]), -1))


def output_block(inputs, allowed):
    query_block, key_block, value_block, log_block = inputs
    weights = jnp.exp(masked_scores(query_block, key_block, allowed) - log_block[..., None]).astype(
        jnp.bfloat16
    )
    return jnp.einsum("fhqk,fkhd->fqhd", weights, value_block, preferred_element_type=jnp.float32)


def back_block(inputs, allowed):
    query_block, grad_block, log_block, inner_block, key_block, value_block = inputs
    probability = jnp.exp(masked_scores(query_block, key_block, allowed) - log_block[..., None])
    grad_prob = jnp.einsum(
        "fqhd,fkhd->fhqk", grad_block, value_block, preferred_element_type=jnp.float32
    )
    grad_score = (probability * (grad_prob - inner_block[..., None])).astype(jnp.bfloat16)
    key_part = (
        jnp.einsum("fhqk,fqhd->fkhd", grad_score, query_block, preferred_element_type=jnp.float32)
        * SCORE_SCALE
    )
    value_part = jnp.einsum(
        "fhqk,fqhd->fkhd",
        probability.astype(jnp.bfloat16),
        grad_block,
        preferred_element_type=jnp.float32,
    )
    query_part = (
        jnp.einsum("fhqk,fkhd->fqhd", grad_score, key_block, preferred_element_type=jnp.float32)
        * SCORE_SCALE
    )
    return (query_part, key_part, value_part)


def general(query_in, key_in, value_in, lookback, out_grad):
    query_rows, key_rows, value_rows = (
        lax.all_to_all(query_in, "tp", split_axis=1, concat_axis=0, tiled=True),
        lax.all_to_all(key_in, "tp", split_axis=1, concat_axis=0, tiled=True),
        lax.all_to_all(value_in, "tp", split_axis=1, concat_axis=0, tiled=True),
    )
    row_count = query_rows.shape[0]
    frame_rows = row_count // (2 * FPC)
    head_count = out_grad.shape[0] // HEAD
    ctx_count = lax.axis_size("ctx")
    group_total = 2 * ctx_count
    device = lax.axis_index("ctx")
    last_device = device == ctx_count - 1
    layout = (2, FPC, frame_rows, head_count, HEAD)
    query_heads = query_rows.reshape(layout)
    grad_heads = out_grad.T.reshape(layout)
    local_pair = jnp.stack([key_rows.reshape(layout), value_rows.reshape(layout)], 4)
    tail_width = head_count * 2 * HEAD
    low_tail = local_pair[0, FPC - W :].reshape(W * frame_rows, tail_width)
    high_tail = local_pair[1, FPC - W :].reshape(W * frame_rows, tail_width)
    below = from_behind(low_tail, "ctx", 1)
    above = from_behind(high_tail, "ctx", -1)
    above = jnp.where(last_device, low_tail, above)
    tails = jnp.stack([below, above]).reshape(2, W, frame_rows, head_count, 2, HEAD)
    extended = jnp.concatenate([tails, local_pair], 1)
    frame_ids = jnp.arange(group_total * FPC, dtype=jnp.int32)
    group_pair = jnp.stack([device, group_total - 1 - device])
    query_frame = group_pair[:, None] * FPC + jnp.arange(FPC, dtype=jnp.int32)[None, :]
    query_look = jnp.sum(jnp.where(query_frame[..., None] == frame_ids, lookback, 0), -1)
    permits = []
    for offset in range(W + 1):
        key_frame = query_frame - W + offset
        permits.append(
            ((key_frame >= 0) & (key_frame >= query_frame - query_look)).reshape(2 * FPC)
        )

    def window(offset):
        pair = extended[:, offset : offset + FPC].reshape(2 * FPC, frame_rows, head_count, 2, HEAD)
        return (pair[:, :, :, 0], pair[:, :, :, 1])

    flat_query = query_heads.reshape(2 * FPC, frame_rows, head_count, HEAD)
    flat_grad = grad_heads.reshape(2 * FPC, frame_rows, head_count, HEAD)
    block_stats = [
        stats_block((flat_query, window(offset)[0]), permits[offset]) for offset in range(W + 1)
    ]
    total_max = reduce(jnp.maximum, [entry[0] for entry in block_stats])
    total_sum = jnp.zeros_like(total_max)
    for entry in block_stats:
        total_sum = total_sum + entry[1] * jnp.exp(entry[0] - total_max)
    log_total = total_max + jnp.log(total_sum)
    summed = jnp.zeros((2 * FPC, frame_rows, head_count, HEAD), jnp.float32)
    for offset in range(W + 1):
        keys, values = window(offset)
        summed = summed + output_block((flat_query, keys, values, log_total), permits[offset])
    attention = summed.astype(jnp.bfloat16)
    inner_sum = jnp.transpose(
        jnp.sum(flat_grad.astype(jnp.float32) * attention.astype(jnp.float32), -1), (0, 2, 1)
    )

    def pad_frames(part, first, stop, length):
        shaped = part.reshape((2, stop - first) + part.shape[1:])
        return jnp.pad(shaped, ((0, 0), (first, length - stop), (0, 0), (0, 0), (0, 0)))

    grad_query = jnp.zeros((2 * FPC, frame_rows, head_count, HEAD), jnp.float32)
    key_total = jnp.zeros((2, W + FPC, frame_rows, head_count, HEAD), jnp.float32)
    value_total = jnp.zeros((2, W + FPC, frame_rows, head_count, HEAD), jnp.float32)
    for offset in range(W + 1):
        keys, values = window(offset)
        query_part, key_part, value_part = back_block(
            (flat_query, flat_grad, log_total, inner_sum, keys, values), permits[offset]
        )
        grad_query = grad_query + query_part
        key_total = key_total + pad_frames(key_part, offset, offset + FPC, W + FPC)
        value_total = value_total + pad_frames(value_part, offset, offset + FPC, W + FPC)
    tail_grads = jnp.stack([key_total[:, :W], value_total[:, :W]], 4).reshape(
        2, W * frame_rows, tail_width
    )
    from_above = from_behind(tail_grads[0].astype(jnp.bfloat16), "ctx", -1).astype(jnp.float32)
    from_below = from_behind(tail_grads[1].astype(jnp.bfloat16), "ctx", 1).astype(jnp.float32)
    returned = jnp.stack(
        [from_above + jnp.where(last_device, tail_grads[1], 0.0), from_below]
    ).reshape(2, W, frame_rows, head_count, 2, HEAD)
    tail_pad = ((0, 0), (FPC - W, 0), (0, 0), (0, 0), (0, 0))
    own_key = key_total[:, W:] + jnp.pad(returned[:, :, :, :, 0], tail_pad)
    own_value = value_total[:, W:] + jnp.pad(returned[:, :, :, :, 1], tail_pad)
    width = head_count * HEAD

    def finish(array):
        return array.astype(jnp.bfloat16).reshape(row_count, width).T

    return (
        attention.reshape(row_count, width).T,
        finish(grad_query),
        finish(own_key),
        finish(own_value),
    )


def solution(mesh):
    tp, ctx = mesh.shape["tp"], mesh.shape["ctx"]
    rows = P(("ctx", "tp"), None)
    out = P("tp", "ctx")

    def step(*args):
        if args[4].shape[0] % PAIR or args[0].shape[0] % CH:
            return general(*args)
        return on_device(tp, ctx, *args)

    return jax.shard_map(
        step,
        mesh=mesh,
        in_specs=(rows, rows, rows, P(), out),
        out_specs=(out,) * 4,
        check_vma=False,
    )
```
